32 devices in a mesh: dp: 8 (over z, y), tensor: 4 (over x, core).
Axes of the slice: x: 2, y: 2, z: 4, core: 2. Of those that a mesh axis runs over, the one named last changes fastest.
Arguments:
- tokens: bfloat16 [8, 512, 768], P('dp'), may hold values from -6 to 6
- cotangent: bfloat16 [8, 512, 768], P('dp'), may hold values from -6 to 6
- norm_gain: float32 [768], replicated, may hold values from 0.1 to 1.9
- w_z: bfloat16 [768, 1536], P(None, 'tensor'), may hold values from -0.21875 to 0.21875
- w_x: bfloat16 [768, 1536], P(None, 'tensor'), may hold values from -0.21875 to 0.21875
- w_bc: bfloat16 [768, 256], replicated, may hold values from -0.21875 to 0.21875
- w_dt: bfloat16 [768, 24], P(None, 'tensor'), may hold values from -0.21875 to 0.21875
- conv_x: float32 [4, 1536], P(None, 'tensor'), may hold values from -3 to 3
- conv_x_bias: float32 [1536], P('tensor'), may hold values from -3 to 3
- conv_bc: float32 [4, 256], replicated, may hold values from -3 to 3
- conv_bc_bias: float32 [256], replicated, may hold values from -3 to 3
- dt_bias: float32 [24], P('tensor'), may hold values from -5 to -1
- a_log: float32 [24], P('tensor'), may hold values from -4 to 2
- d_skip: float32 [24], P('tensor'), may hold values from 0.5 to 2
- gate_gain: float32 [1536], P('tensor'), may hold values from 0.1 to 1.9
- w_out: bfloat16 [1536, 768], P('tensor'), may hold values from -0.15625 to 0.15625
Outputs:
- result: bfloat16 [8, 512, 768], P('dp')
- grad_x: bfloat16 [8, 512, 768], P('dp')
- grad_norm_gain: float32 [768], replicated
- grad_w_z: float32 [768, 1536], P(None, 'tensor')
- grad_w_x: float32 [768, 1536], P(None, 'tensor')
- grad_w_bc: float32 [768, 256], replicated
- grad_w_dt: float32 [768, 24], P(None, 'tensor')
- grad_conv_x: float32 [4, 1536], P(None, 'tensor')
- grad_conv_x_bias: float32 [1536], P('tensor')
- grad_conv_bc: float32 [4, 256], replicated
- grad_conv_bc_bias: float32 [256], replicated
- grad_dt_bias: float32 [24], P('tensor')
- grad_a_log: float32 [24], P('tensor')
- grad_d_skip: float32 [24], P('tensor')
- grad_gate_gain: float32 [1536], P('tensor')
- grad_w_out: float32 [1536, 768], P('tensor')
The draws below stay inside these ranges and needn't reach their ends.
All inputs are finite; a program needn't handle non-finite values.
Results may differ from the reference program's by a relative error of at most 0.013.
Values may be sent and summed in bfloat16 or wider, within the bound.
A program may use at most 128 MiB of HBM per device.

```python
import jax
import jax.numpy as jnp
from jax import lax

D = 768
H = 24
N = 128
K = 4
Q = 256
L = 512
DI = 1536
SEQS = 8


def shard_levels(stream_key, dims, cuts, least, high):
    def one(dim, blocks):
        steps = jax.random.uniform(jax.random.fold_in(jax.random.fold_in(stream_key, 6), dim), (blocks,), jnp.float32, least / len(cuts), high / len(cuts))
        return jnp.repeat(jnp.exp(steps), dims[dim] // blocks).reshape((-1,) + (1,) * (len(dims) - dim - 1))

    level = one(*cuts[0])
    for cut in cuts[1:]:
        level = level * one(*cut)
    return level


def centred(stream_key, dims, width, reach, split=(), held_as=jnp.bfloat16):
    level = shard_levels(stream_key, dims, split, -0.22, 0.18) if split else 1.0
    values = jax.random.normal(stream_key, dims, jnp.float32) * width * level
    return jnp.minimum(jnp.maximum(values, -reach), reach).astype(held_as)


def setup_inputs(seed: int = 0) -> dict:
    key_list = jax.random.split(jax.random.key(seed), 17)
    tokens = centred(key_list[0], (SEQS, L, D), 1.0, 6.0, ((0, 8),))
    cotangent = centred(key_list[1], (SEQS, L, D), 1.0, 6.0, ((0, 8),))
    norm_gain = jnp.clip(1.0 + 0.18 * jax.random.normal(key_list[2], (D,), jnp.float32), 0.1, 1.9)
    w_z = centred(key_list[3], (D, DI), D ** -0.5, 0.21875, ((1, 4),))
    w_x = centred(key_list[4], (D, DI), D ** -0.5, 0.21875, ((1, 4),))
    w_bc = centred(key_list[5], (D, 2 * N), D ** -0.5, 0.21875)
    w_dt = centred(key_list[6], (D, H), D ** -0.5, 0.21875, ((1, 4),))
    conv_x = centred(key_list[7], (K, DI), K ** -0.5, 3.0, ((1, 4),), jnp.float32)
    conv_x_bias = centred(key_list[8], (DI,), 0.5, 3.0, ((0, 4),), jnp.float32)
    conv_bc = centred(key_list[9], (K, 2 * N), K ** -0.5, 3.0, (), jnp.float32)
    conv_bc_bias = centred(key_list[10], (2 * N,), 0.5, 3.0, (), jnp.float32)
    dt_bias = jnp.clip(-5.0 + 4.0 * jax.random.uniform(key_list[11], (H,), jnp.float32) ** shard_levels(key_list[11], (H,), ((0, 4),), -0.2, 0.2), -5.0, -1.0)
    a_log = jnp.clip(-4.0 + 6.0 * jax.random.uniform(key_list[12], (H,), jnp.float32) ** shard_levels(key_list[12], (H,), ((0, 4),), -0.2, 0.2), -4.0, 2.0)
    d_skip = jnp.clip(0.5 + 1.5 * jax.random.uniform(key_list[13], (H,), jnp.float32) ** shard_levels(key_list[13], (H,), ((0, 4),), -0.2, 0.2), 0.5, 2.0)
    gate_gain = jnp.clip(1.0 + 0.18 * jax.random.normal(key_list[14], (DI,), jnp.float32), 0.1, 1.9)
    w_out = centred(key_list[15], (DI, D), DI ** -0.5, 0.15625, ((0, 4),))
    return {"tokens": tokens, "cotangent": cotangent, "norm_gain": norm_gain, "w_z": w_z, "w_x": w_x, "w_bc": w_bc, "w_dt": w_dt, "conv_x": conv_x, "conv_x_bias": conv_x_bias, "conv_bc": conv_bc, "conv_bc_bias": conv_bc_bias, "dt_bias": dt_bias, "a_log": a_log, "d_skip": d_skip, "gate_gain": gate_gain, "w_out": w_out}


epsilon = 1e-05
highest = lax.Precision.HIGHEST

def input_norm(values, norm_gain):
    return values * lax.rsqrt(lax.optimization_barrier(jnp.mean(values * values, axis=-1, keepdims=True)) + epsilon) * norm_gain[None, :]

def causal_conv(values, kernel, shift_bias):
    length = values.shape[0]
    kernel_taps = kernel.shape[0]
    padded = jnp.pad(values, ((kernel_taps - 1, 0), (0, 0)))
    summed = jnp.zeros_like(values) + shift_bias[None, :]
    for offset in range(kernel_taps):
        summed = summed + kernel[offset][None, :] * padded[offset:offset + length]
    return summed

def state_scan(xheads, b_rows, c_rows, step_size, log_decay):
    length, head_count, head_dim = xheads.shape
    blocks = length // Q
    states = b_rows.shape[1]
    causal_mask = jnp.arange(Q)[:, None] >= jnp.arange(Q)[None, :]

    def advance(carried_state, pieces):
        x_blk, b_blk, c_blk, dt_blk, a_blk = pieces
        cumulative = jnp.cumsum(a_blk, axis=0)
        spread = jnp.where(causal_mask[:, :, None], cumulative[:, None, :] - cumulative[None, :, :], -jnp.inf)
        scores = jnp.dot(c_blk, b_blk.T, precision=highest)
        mixing = scores[:, :, None] * jnp.exp(spread) * dt_blk[None, :, :]
        inside = jnp.einsum('tsh,shp->thp', mixing, x_blk, precision=highest)
        carried = jnp.einsum('tn,hpn->thp', c_blk, carried_state, precision=highest) * jnp.exp(cumulative)[:, :, None]
        weight_tail = jnp.exp(cumulative[-1][None, :] - cumulative) * dt_blk
        update = jnp.einsum('shp,sn->hpn', x_blk * weight_tail[:, :, None], b_blk, precision=highest)
        carried_state = carried_state * jnp.exp(cumulative[-1])[:, None, None] + update
        return (carried_state, inside + carried)
    initial = jnp.zeros((head_count, head_dim, states), jnp.float32)
    pieces = (xheads.reshape(blocks, Q, head_count, head_dim), b_rows.reshape(blocks, Q, states), c_rows.reshape(blocks, Q, states), step_size.reshape(blocks, Q, head_count), log_decay.reshape(blocks, Q, head_count))
    _, outputs = lax.scan(advance, initial, pieces)
    return outputs.reshape(length, head_count, head_dim)

def mixer(x_pre, bc_pre, dt_pre, conv_x, conv_x_bias, conv_bc, conv_bc_bias, dt_bias, a_log, d_skip):
    length, head_count = dt_pre.shape
    xconv = jax.nn.silu(causal_conv(x_pre, conv_x, conv_x_bias))
    bcconv = jax.nn.silu(causal_conv(bc_pre, conv_bc, conv_bc_bias))
    states = bc_pre.shape[1] // 2
    step_size = jax.nn.softplus(dt_pre + dt_bias[None, :])
    log_decay = -step_size * jnp.exp(a_log)[None, :]
    xheads = xconv.reshape(length, head_count, -1)
    mixed = state_scan(xheads, bcconv[:, :states], bcconv[:, states:], step_size, log_decay)
    mixed = mixed + d_skip[None, :, None] * xheads
    return mixed.reshape(length, -1)

def silu_slope(values):
    sigmoid = jax.nn.sigmoid(values)
    return sigmoid * (1.0 + values * (1.0 - sigmoid))

def contract_rows(left, right):
    return lax.dot_general(left, right, (((0,), (0,)), ((), ())), preferred_element_type=jnp.float32)

def contract_cols(left, right):
    return lax.dot_general(left, right, (((1,), (1,)), ((), ())), preferred_element_type=jnp.float32)

def sequence_pass(sequence, cotan, norm_gain, w_z, w_x, w_bc, w_dt, conv_x, conv_x_bias, conv_bc, conv_bc_bias, dt_bias, a_log, d_skip, gate_gain, w_out):
    widef = sequence.astype(jnp.float32)
    normed_f, norm_back = jax.vjp(input_norm, widef, norm_gain)
    normed = normed_f.astype(jnp.bfloat16)
    gate_pre = jnp.dot(normed, w_z, preferred_element_type=jnp.float32)
    x_pre = jnp.dot(normed, w_x, preferred_element_type=jnp.float32)
    bc_pre = jnp.dot(normed, w_bc, preferred_element_type=jnp.float32)
    dt_pre = jnp.dot(normed, w_dt, preferred_element_type=jnp.float32)
    mixed, mixer_back = jax.vjp(mixer, x_pre, bc_pre, dt_pre, conv_x, conv_x_bias, conv_bc, conv_bc_bias, dt_bias, a_log, d_skip)
    gate_act = jax.nn.silu(gate_pre)
    gated = mixed * gate_act
    inverse = lax.rsqrt(lax.optimization_barrier(jnp.mean(gated * gated, axis=-1, keepdims=True)) + epsilon)
    gated_n = (gated * inverse * gate_gain[None, :]).astype(jnp.bfloat16)
    result = (widef + jnp.dot(gated_n, w_out, preferred_element_type=jnp.float32)).astype(jnp.bfloat16)
    grad_w_out = contract_rows(gated_n, cotan)
    d_gated_n = contract_cols(cotan, w_out)
    grad_gate_gain = lax.optimization_barrier(jnp.sum(d_gated_n * gated * inverse, axis=0))
    scaled = gate_gain[None, :] * d_gated_n
    d_gated = inverse * scaled - gated * inverse ** 3 * lax.optimization_barrier(jnp.mean(scaled * gated, axis=-1, keepdims=True))
    d_mixed = d_gated * gate_act
    d_gate_pre = d_gated * mixed * silu_slope(gate_pre)
    back = mixer_back(d_mixed)
    d_gate_b = d_gate_pre.astype(jnp.bfloat16)
    d_x_b = back[0].astype(jnp.bfloat16)
    d_bc_b = back[1].astype(jnp.bfloat16)
    d_dt_b = back[2].astype(jnp.bfloat16)
    grad_w_z = contract_rows(normed, d_gate_b)
    grad_w_x = contract_rows(normed, d_x_b)
    grad_w_bc = contract_rows(normed, d_bc_b)
    grad_w_dt = contract_rows(normed, d_dt_b)
    d_normed = contract_cols(d_gate_b, w_z) + contract_cols(d_x_b, w_x) + contract_cols(d_bc_b, w_bc) + contract_cols(d_dt_b, w_dt)
    d_tokens, grad_norm_gain = norm_back(d_normed)
    grad_x = (cotan.astype(jnp.float32) + d_tokens).astype(jnp.bfloat16)
    grads = (grad_norm_gain, grad_w_z, grad_w_x, grad_w_bc, grad_w_dt, back[3], back[4], back[5], back[6], back[7], back[8], back[9], grad_gate_gain, grad_w_out)
    return (result, grad_x, grads)

def reference(tokens, cotangent, norm_gain, w_z, w_x, w_bc, w_dt, conv_x, conv_x_bias, conv_bc, conv_bc_bias, dt_bias, a_log, d_skip, gate_gain, w_out):
    params = (norm_gain, w_z, w_x, w_bc, w_dt, conv_x, conv_x_bias, conv_bc, conv_bc_bias, dt_bias, a_log, d_skip, gate_gain, w_out)
    zero_grads = (jnp.zeros(norm_gain.shape, jnp.float32), jnp.zeros(w_z.shape, jnp.float32), jnp.zeros(w_x.shape, jnp.float32), jnp.zeros(w_bc.shape, jnp.float32), jnp.zeros(w_dt.shape, jnp.float32), jnp.zeros(conv_x.shape, jnp.float32), jnp.zeros(conv_x_bias.shape, jnp.float32), jnp.zeros(conv_bc.shape, jnp.float32), jnp.zeros(conv_bc_bias.shape, jnp.float32), jnp.zeros(dt_bias.shape, jnp.float32), jnp.zeros(a_log.shape, jnp.float32), jnp.zeros(d_skip.shape, jnp.float32), jnp.zeros(gate_gain.shape, jnp.float32), jnp.zeros(w_out.shape, jnp.float32))

    def visit(totals, pair):
        result, grad_x, grads = sequence_pass(pair[0], pair[1], *params)
        totals = tuple((left + right for left, right in zip(totals, grads)))
        return (totals, (result, grad_x))
    totals, (results, grads_x) = lax.scan(visit, zero_grads, (tokens, cotangent))
    return (results, grads_x) + totals
```

```python
import functools

import jax
import jax.numpy as jnp
from jax import lax
from jax.experimental import pallas as pl
from jax.experimental.pallas import tpu as pltpu
from jax.sharding import PartitionSpec as P

Q = 256
LANES = 128
HEAD = 8
epsilon = 1e-05
highest = lax.Precision.HIGHEST
f32 = jnp.float32
bf16 = jnp.bfloat16
NN = ((1,), (0,))
NT = ((1,), (1,))
TN = ((0,), (0,))


def mm(a, b, dims=NN):
    return lax.dot_general(
        a.astype(bf16), b.astype(bf16), (dims, ((), ())), preferred_element_type=f32
    )


def exact(a, b, dims=NN):
    return lax.dot_general(a, b, (dims, ((), ())), precision=highest, preferred_element_type=f32)


def iota(shape, dim):
    return lax.broadcasted_iota(jnp.int32, shape, dim)


def spread_matrix(width, head_dim):
    return (iota((LANES, width), 1) // head_dim == iota((LANES, width), 0)).astype(f32)


def spread_rows(width, head_dim):
    return (iota((width, LANES), 0) // head_dim == iota((width, LANES), 1)).astype(f32)


def shifted(pad_ref, start, kernel_ref, bias_ref):
    taps = kernel_ref.shape[0]
    total = bias_ref[...] + jnp.zeros((Q, pad_ref.shape[1]), f32)
    for j in range(taps):
        total = total + kernel_ref[j : j + 1, :] * pad_ref[pl.ds(HEAD + start - taps + 1 + j, Q), :]
    return total


def softplus(v):
    return jnp.maximum(v, 0.0) + jnp.log1p(jnp.exp(-jnp.abs(v)))


def decays(dt_rows, hp_ref):
    pre = dt_rows + hp_ref[0:1, :]
    step = softplus(pre)
    rate = jnp.exp(hp_ref[1:2, :])
    log_decay = -step * rate
    lower = (iota((Q, Q), 0) >= iota((Q, Q), 1)).astype(f32)
    return pre, step, rate, log_decay, exact(lower, log_decay)


def kernel_front(
    heads, tok, cot, ng, wz, wx, wbd, cx, cxb, cbc, cbcb, hp, gg, wo,
    normed_o, gate_o, x_o, bc_o, dt_o, cum_o, state_o, mixed_o, dgn_o, stats_o,
):
    length, inner = mixed_o.shape
    states = cbc.shape[1] // 2
    head_dim = inner // heads
    per = LANES // head_dim
    spread = spread_matrix(inner, head_dim)
    x_o[0:HEAD, :] = jnp.zeros((HEAD, inner), f32)
    bc_o[0:HEAD, :] = jnp.zeros((HEAD, 2 * states), f32)
    causal = iota((Q, Q), 0) >= iota((Q, Q), 1)
    lane = iota((Q, LANES), 1)
    chunks = length // Q
    for c in range(chunks):
        rows = pl.ds(c * Q, Q)
        t = tok[rows, :].astype(f32)
        n = t * lax.rsqrt(jnp.mean(t * t, axis=-1, keepdims=True) + epsilon) * ng[...]
        n = n.astype(bf16)
        normed_o[rows, :] = n
        gate_o[rows, :] = mm(n, wz[...])
        x_o[pl.ds(HEAD + c * Q, Q), :] = mm(n, wx[...])
        bd = mm(n, wbd[...])
        bc_o[pl.ds(HEAD + c * Q, Q), :] = bd[:, : 2 * states]
        dt_o[rows, :] = bd[:, 2 * states :]
        dgn_o[rows, :] = mm(cot[rows, :], wo[...], NT)
    state_o[0] = jnp.zeros((inner, states), f32)
    for c in range(chunks):
        rows = pl.ds(c * Q, Q)
        v = shifted(x_o, c * Q, cx, cxb)
        xc = v * jax.nn.sigmoid(v)
        v = shifted(bc_o, c * Q, cbc, cbcb)
        bcc = v * jax.nn.sigmoid(v)
        b = bcc[:, :states].astype(bf16)
        cc = bcc[:, states:].astype(bf16)
        _, step, _, _, cum = decays(dt_o[rows, :], hp)
        cum_o[rows, :] = cum
        cum_t = jnp.transpose(cum)
        u = xc * exact(step, spread)
        scores = mm(cc, b, NT)
        outs = []
        for g in range(inner // LANES):
            part = u[:, g * LANES : (g + 1) * LANES]
            acc = jnp.zeros((Q, LANES), f32)
            for k in range(per):
                h = g * per + k
                e = jnp.exp(jnp.where(causal, cum[:, h : h + 1] - cum_t[h : h + 1, :], -1e30))
                acc = acc + mm(scores * e, jnp.where(lane // head_dim == k, part, 0.0))
            outs.append(acc)
        mixed = jnp.concatenate(outs, axis=1)
        if c > 0:
            mixed = mixed + mm(cc, state_o[c], NT) * exact(jnp.exp(cum), spread)
        if c + 1 < chunks:
            last = cum[Q - 1 : Q, :]
            tail = u * exact(jnp.exp(last - cum), spread)
            update = mm(tail, b, TN)
            if c > 0:
                rowdec = jnp.sum(
                    spread_rows(inner, head_dim) * jnp.exp(last), axis=1, keepdims=True
                )
                update = update + state_o[c] * rowdec
            state_o[c + 1] = update
        skip = jnp.sum(spread * hp_skip_col(hp), axis=0, keepdims=True)
        mixed = mixed + skip * xc
        mixed_o[rows, :] = mixed
        gate = gate_o[rows, :]
        gated = mixed * (gate * jax.nn.sigmoid(gate))
        sq = jnp.sum(gated * gated, axis=1, keepdims=True)
        pr = jnp.sum(gg[...] * dgn_o[rows, :] * gated, axis=1, keepdims=True)
        both = jnp.where(lane == 0, sq, jnp.where(lane == 1, pr, 0.0))
        stats_o[:, c * Q : (c + 1) * Q] = jnp.transpose(both)[0:8, :]


def hp_skip_col(hp):
    wide = jnp.where(iota((LANES, LANES), 0) == iota((LANES, LANES), 1), hp[2:3, :], 0.0)
    return jnp.sum(wide, axis=1, keepdims=True)


def put_rows(ref, start, value):
    count = value.shape[1] // LANES
    for r in range(value.shape[0]):
        for k in range(count):
            at = start + r * count + k
            ref[at : at + 1, :] = value[r : r + 1, k * LANES : (k + 1) * LANES]
    return start + value.shape[0] * count


def kernel_back(
    heads, inner_total, tok, cot, ng, wz, wx, wbd, cx, cxb, cbc, cbcb, hp, gg, wo,
    normed, gate_r, x_r, bc_r, dt_r, cum_r, state_r, mixed_r, dgn_r, stats,
    res_o, dn_o, gz_o, gx_o, gwo_o, gbc_o, sm_o, smt_o,
    gn_s, dz_s, dx_s, dbd_s, dvx_s, dvbc_s, inv_s,
):
    length, inner = mixed_r.shape
    states = cbc.shape[1] // 2
    head_dim = inner // heads
    per = LANES // head_dim
    taps = cx.shape[0]
    spread = spread_matrix(inner, head_dim)
    spread_r = spread_rows(inner, head_dim)
    causal = iota((Q, Q), 0) >= iota((Q, Q), 1)
    lower = causal.astype(f32)
    lane = iota((Q, LANES), 1)
    skip = jnp.sum(spread * hp_skip_col(hp), axis=0, keepdims=True)
    dvx_s[pl.ds(length, HEAD), :] = jnp.zeros((HEAD, inner), f32)
    dvbc_s[pl.ds(length, HEAD), :] = jnp.zeros((HEAD, 2 * states), f32)
    chunks = length // Q
    for c in range(chunks):
        block = jnp.concatenate(
            [stats[:, c * Q : (c + 1) * Q], jnp.zeros((LANES - 8, Q), f32)], axis=0
        )
        inv_s[pl.ds(c * Q, Q), :] = jnp.transpose(block)
    g_gain = jnp.zeros((1, inner), f32)
    g_skip = jnp.zeros((1, inner), f32)
    g_alog = jnp.zeros((1, LANES), f32)
    g_dtb = jnp.zeros((1, LANES), f32)
    g_cx = [jnp.zeros((1, inner), f32) for _ in range(taps)]
    g_cxb = jnp.zeros((1, inner), f32)
    g_cbc = [jnp.zeros((1, 2 * states), f32) for _ in range(taps)]
    g_cbcb = jnp.zeros((1, 2 * states), f32)
    d_state = None
    for c in reversed(range(chunks)):
        rows = pl.ds(c * Q, Q)
        gate = gate_r[rows, :]
        mixed = mixed_r[rows, :]
        sg = jax.nn.sigmoid(gate)
        act = gate * sg
        gated = mixed * act
        inv = lax.rsqrt(inv_s[rows, :][:, 0:1] / inner_total + epsilon)
        pm = inv_s[rows, :][:, 1:2] / inner_total
        dgn = dgn_r[rows, :]
        normal = gated * inv
        gn_s[rows, :] = (normal * gg[...]).astype(bf16)
        g_gain = g_gain + jnp.sum(dgn * normal, axis=0, keepdims=True)
        dg = inv * (gg[...] * dgn) - gated * (inv * inv * inv) * pm
        dy = dg * act
        dz_s[rows, :] = (dg * mixed * (sg * (1.0 + gate * (1.0 - sg)))).astype(bf16)

        vx = shifted(x_r, c * Q, cx, cxb)
        sx = jax.nn.sigmoid(vx)
        xc = vx * sx
        vb = shifted(bc_r, c * Q, cbc, cbcb)
        sb = jax.nn.sigmoid(vb)
        bcc = vb * sb
        b = bcc[:, :states].astype(bf16)
        cc = bcc[:, states:].astype(bf16)
        pre = dt_r[rows, :] + hp[0:1, :]
        step = softplus(pre)
        rate = jnp.exp(hp[1:2, :])
        log_decay = -step * rate
        cum = cum_r[rows, :]
        cum_t = jnp.transpose(cum)
        stepw = exact(step, spread)
        u = xc * stepw
        scores = mm(cc, b, NT)
        d_scores = jnp.zeros((Q, Q), f32)
        d_cum = jnp.zeros((Q, LANES), f32)
        cols = jnp.zeros((8, Q), f32)
        dus = []
        for g in range(inner // LANES):
            up = u[:, g * LANES : (g + 1) * LANES].astype(bf16)
            dyp = dy[:, g * LANES : (g + 1) * LANES]
            acc = jnp.zeros((Q, LANES), f32)
            for k in range(per):
                h = g * per + k
                e = jnp.exp(jnp.where(causal, cum[:, h : h + 1] - cum_t[h : h + 1, :], -1e30))
                p = scores * e
                dyh = jnp.where(lane // head_dim == k, dyp, 0.0).astype(bf16)
                dp = mm(dyh, up, NT)
                d_scores = d_scores + dp * e
                gp = dp * p
                d_cum = d_cum + jnp.where(lane == h, jnp.sum(gp, axis=1, keepdims=True), 0.0)
                cols = cols + jnp.where(
                    iota((8, Q), 0) == h, jnp.sum(gp, axis=0, keepdims=True), 0.0
                )
                acc = acc + mm(p, dyh, TN)
            dus.append(acc)
        du = jnp.concatenate(dus, axis=1)
        d_cum = d_cum - jnp.transpose(
            jnp.concatenate([cols, jnp.zeros((LANES - 8, Q), f32)], axis=0)
        )
        d_c = mm(d_scores, b)
        d_b = mm(d_scores, cc, TN)
        d_prev = None
        if c > 0:
            state = state_r[c]
            decayed = exact(jnp.exp(cum), spread)
            dz = dy * decayed
            carried = mm(cc, state, NT) * dz
            d_cum = d_cum + exact(carried, spread, NT)
            d_c = d_c + mm(dz, state)
            d_prev = mm(dz, cc, TN)
        if d_state is not None:
            last = cum[Q - 1 : Q, :]
            tailw = exact(jnp.exp(last - cum), spread)
            ut = u * tailw
            dut = mm(b, d_state, NT)
            d_b = d_b + mm(ut, d_state)
            du = du + dut * tailw
            q = exact(dut * ut, spread, NT)
            d_last = jnp.sum(q, axis=0, keepdims=True)
            if c > 0:
                rowdec = jnp.sum(spread_r * jnp.exp(last), axis=1, keepdims=True)
                r = jnp.sum(d_state * state_r[c], axis=1, keepdims=True) * rowdec
                d_last = d_last + jnp.sum(spread_r * r, axis=0, keepdims=True)
                d_prev = d_prev + d_state * rowdec
            d_cum = d_cum - q + jnp.where(iota((Q, LANES), 0) == Q - 1, d_last, 0.0)
        d_state = d_prev
        d_log = exact(lower, d_cum, TN)
        g_alog = g_alog + jnp.sum(d_log * log_decay, axis=0, keepdims=True)
        d_step = exact(du * xc, spread, NT) - d_log * rate
        d_pre = d_step * jax.nn.sigmoid(pre)
        d_pre = jnp.where(lane < heads, d_pre, 0.0)
        g_dtb = g_dtb + jnp.sum(d_pre, axis=0, keepdims=True)
        g_skip = g_skip + jnp.sum(dy * xc, axis=0, keepdims=True)
        dxc = du * stepw + skip * dy
        dvx = dxc * (sx * (1.0 + vx * (1.0 - sx)))
        dvb = jnp.concatenate([d_b, d_c], axis=1) * (sb * (1.0 + vb * (1.0 - sb)))
        dvx_s[rows, :] = dvx
        dvbc_s[rows, :] = dvb
        g_cxb = g_cxb + jnp.sum(dvx, axis=0, keepdims=True)
        g_cbcb = g_cbcb + jnp.sum(dvb, axis=0, keepdims=True)
        dx = jnp.zeros((Q, inner), f32)
        dbc = jnp.zeros((Q, 2 * states), f32)
        for j in range(taps):
            back = pl.ds(c * Q + taps - 1 - j, Q)
            ahead = pl.ds(HEAD + c * Q - taps + 1 + j, Q)
            dx = dx + cx[j : j + 1, :] * dvx_s[back, :]
            dbc = dbc + cbc[j : j + 1, :] * dvbc_s[back, :]
            g_cx[j] = g_cx[j] + jnp.sum(dvx * x_r[ahead, :], axis=0, keepdims=True)
            g_cbc[j] = g_cbc[j] + jnp.sum(dvb * bc_r[ahead, :], axis=0, keepdims=True)
        dx_s[rows, :] = dx.astype(bf16)
        dbd_s[rows, :] = jnp.concatenate([dbc, d_pre], axis=1).astype(bf16)

    g_ng = jnp.zeros((1, tok.shape[1]), f32)
    for c in range(chunks):
        rows = pl.ds(c * Q, Q)
        res_o[rows, :] = mm(gn_s[rows, :], wo[...]).astype(bf16)
        dn = mm(dz_s[rows, :], wz[...], NT) + mm(dx_s[rows, :], wx[...], NT)
        dn = dn + mm(dbd_s[rows, :], wbd[...], NT)
        dn_o[rows, :] = dn.astype(bf16)
        t = tok[rows, :].astype(f32)
        unit = t * lax.rsqrt(jnp.mean(t * t, axis=-1, keepdims=True) + epsilon)
        g_ng = g_ng + jnp.sum(dn * unit, axis=0, keepdims=True)
    gz_o[...] = mm(normed[...], dz_s[...], TN).astype(bf16)
    gx_o[...] = mm(normed[...], dx_s[...], TN).astype(bf16)
    gwo_o[...] = mm(gn_s[...], cot[...], TN).astype(bf16)
    gb = mm(normed[...], dbd_s[:, : 2 * states], TN).astype(bf16)
    width = gb.shape[0]
    for k in range(2 * states // LANES):
        gbc_o[pl.ds(k * width, width), :] = gb[:, k * LANES : (k + 1) * LANES]
    gdt = mm(dbd_s[:, 2 * states :], normed[...], TN)
    sm_o[...] = jnp.zeros(sm_o.shape, f32)
    smt_o[...] = jnp.zeros(smt_o.shape, f32)
    at = put_rows(sm_o, 0, gdt[0:heads, :])
    for row in (*g_cx, g_cxb, g_gain):
        at = put_rows(sm_o, at, row)
    for row in (g_dtb, g_alog, exact(g_skip, spread, NT)):
        at = put_rows(sm_o, at, row)
    at = 0
    for row in (*g_cbc, g_cbcb, g_ng):
        at = put_rows(smt_o, at, row)


class Stream:
    def __init__(self, src, bits):
        rows, self.lanes = src.shape
        self.rows, self.dtype, self.bits = rows, src.dtype, bits
        tile = 32 // jnp.dtype(src.dtype).itemsize
        self.halve = []
        for _ in bits:
            split = rows % (2 * tile) == 0
            self.halve.append(split)
            if split:
                rows //= 2
        self.copies = len(bits) + sum(self.halve)

    def scratch(self):
        rows, shapes = self.rows, []
        shapes.append(pltpu.VMEM((self.rows, self.lanes), self.dtype))
        shapes.append(pltpu.VMEM((self.rows, self.lanes), self.dtype))
        shapes.append(pltpu.SemaphoreType.DMA((self.copies,)))
        shapes.append(pltpu.SemaphoreType.DMA((self.copies,)))
        for split in self.halve:
            if split:
                rows //= 2
            shapes.append(pltpu.VMEM((rows, self.lanes), self.dtype))
        return shapes


def run_stream(stream, src, refs):
    acc, out, send, recv = refs[:4]
    slots = refs[4:]
    off, size, ref = 0, stream.rows, src
    trail = []
    sem = 0
    tile = 32 // jnp.dtype(stream.dtype).itemsize

    def place(v):
        return v if isinstance(v, int) else pl.multiple_of(v, tile)

    last = len(stream.bits) - 1
    for k, ((axis, bit), split) in enumerate(zip(stream.bits, stream.halve)):
        me = lax.axis_index(axis)
        side = lax.rem(me // bit, 2)
        peer = me + bit - 2 * bit * side
        if split:
            half = size // 2
            keep, give = off + side * half, off + (1 - side) * half
            trail.append((axis, peer, off))
        else:
            half, keep, give = size, off, off
        copy = pltpu.make_async_remote_copy(
            src_ref=ref.at[pl.ds(place(give), half), :],
            dst_ref=slots[k],
            send_sem=send.at[sem],
            recv_sem=recv.at[sem],
            device_id={axis: peer},
            device_id_type=pl.DeviceIdType.MESH,
        )
        sem += 1
        copy.start()
        yield
        copy.wait()
        rows = pl.ds(place(keep), half)
        target = out if k == last else acc
        total = ref[rows, :].astype(f32) + slots[k][...].astype(f32)
        target[rows, :] = total.astype(stream.dtype)
        off, size, ref = keep, half, target
    for axis, peer, parent in reversed(trail):
        rows = pl.ds(place(off), size)
        copy = pltpu.make_async_remote_copy(
            src_ref=out.at[rows, :],
            dst_ref=out.at[rows, :],
            send_sem=send.at[sem],
            recv_sem=recv.at[sem],
            device_id={axis: peer},
            device_id_type=pl.DeviceIdType.MESH,
        )
        sem += 1
        copy.start()
        yield
        copy.wait()
        off, size = parent, size * 2


def greet(peers):
    barrier = pltpu.get_barrier_semaphore()
    for axis, bit in peers:
        me = lax.axis_index(axis)
        peer = me + bit - 2 * bit * lax.rem(me // bit, 2)
        pl.semaphore_signal(
            barrier, inc=1, device_id={axis: peer}, device_id_type=pl.DeviceIdType.MESH
        )
    pl.semaphore_wait(barrier, len(peers))


def run_all(streams, sources, scratch):
    running = []
    at = 0
    outs = []
    for stream, src in zip(streams, sources):
        count = 4 + len(stream.bits)
        refs = scratch[at : at + count]
        at += count
        outs.append(refs[1])
        running.append(run_stream(stream, src, refs))
    while running:
        running = [r for r in running if next(r, 1) is None]
    return outs


def kernel_stats(streams, peers, src, out, *scratch):
    greet(peers)
    (total,) = run_all(streams, [src], scratch)
    out[...] = total[...]


def kernel_sums(
    streams, peers, tok, cot, ng, res, dn, gz, gx, gwo, gbc, sm, smt,
    res_o, gt_o, gz_o, gx_o, gwo_o, gbc_o, sm_o, smt_o, *scratch,
):
    greet(peers)
    a_res, a_dn, a_gz, a_gx, a_gwo, a_gbc, a_sm, a_smt = run_all(
        streams, [res, dn, gz, gx, gwo, gbc, sm, smt], scratch
    )
    for c in range(tok.shape[0] // Q):
        rows = pl.ds(c * Q, Q)
        t = tok[rows, :].astype(f32)
        res_o[rows, :] = (t + a_res[rows, :].astype(f32)).astype(bf16)
        r = lax.rsqrt(jnp.mean(t * t, axis=-1, keepdims=True) + epsilon)
        gd = a_dn[rows, :].astype(f32) * ng[...]
        mean = jnp.mean(t * gd, axis=-1, keepdims=True)
        d = r * gd - t * (r * r * r) * mean
        gt_o[rows, :] = (cot[rows, :].astype(f32) + d).astype(bf16)
    gz_o[...] = a_gz[...].astype(f32)
    gx_o[...] = a_gx[...].astype(f32)
    gwo_o[...] = a_gwo[...].astype(f32)
    width = gbc_o.shape[0]
    for k in range(gbc_o.shape[1] // LANES):
        gbc_o[:, k * LANES : (k + 1) * LANES] = a_gbc[pl.ds(k * width, width), :].astype(f32)
    sm_o[...] = a_sm[...]
    smt_o[...] = a_smt[...]


def call(body, args, outs, scratch=(), **params):
    vmem = pl.BlockSpec(memory_space=pltpu.VMEM)
    return pl.pallas_call(
        body,
        out_shape=[jax.ShapeDtypeStruct(s, d) for s, d in outs],
        in_specs=[vmem] * len(args),
        out_specs=[vmem] * len(outs),
        scratch_shapes=list(scratch),
        compiler_params=pltpu.CompilerParams(vmem_limit_bytes=60 * 1024 * 1024, **params),
    )(*args)


def per_device(
    tokens, cotangent, norm_gain, w_z, w_x, w_bc, w_dt, conv_x, conv_x_bias, conv_bc,
    conv_bc_bias, dt_bias, a_log, d_skip, gate_gain, w_out,
):
    seqs, length, width = tokens.shape
    assert seqs == 1 and length % Q == 0
    heads = dt_bias.shape[0]
    inner = w_z.shape[1]
    wide = w_bc.shape[1]
    states = wide // 2
    taps = conv_x.shape[0]
    dp, tensor = lax.axis_size("dp"), lax.axis_size("tensor")
    inner_total = inner * tensor
    chunks = length // Q
    tok = tokens.reshape(length, width)
    cot = cotangent.reshape(length, width)
    wbd = jnp.concatenate([w_bc, jnp.pad(w_dt, ((0, 0), (0, LANES - heads)))], axis=1)
    hp = jnp.pad(jnp.stack([dt_bias, a_log, d_skip]), ((0, 5), (0, LANES - heads)))
    shared = (
        tok, cot, norm_gain[None, :], w_z, w_x, wbd, conv_x, conv_x_bias[None, :], conv_bc,
        conv_bc_bias[None, :], hp, gate_gain[None, :], w_out,
    )
    kept = call(
        functools.partial(kernel_front, heads),
        shared,
        [
            ((length, width), bf16),
            ((length, inner), f32),
            ((length + HEAD, inner), f32),
            ((length + HEAD, wide), f32),
            ((length, LANES), f32),
            ((length, LANES), f32),
            ((chunks, inner, states), f32),
            ((length, inner), f32),
            ((length, inner), f32),
            ((8, length), f32),
        ],
    )
    t_bits = [("tensor", 1 << k) for k in range(tensor.bit_length() - 1)]
    d_bits = [("dp", 1 << k) for k in range(dp.bit_length() - 1)]
    stats = kept[-1]
    stream = Stream(stats, t_bits)
    (stats,) = call(
        functools.partial(kernel_stats, [stream], t_bits),
        (stats,),
        [(stats.shape, f32)],
        stream.scratch(),
        collective_id=0,
        has_side_effects=True,
    )
    sm_rows = heads * width // LANES + (taps + 2) * inner // LANES + 3
    unit = 8 * dp
    sm_rows = -(-sm_rows // unit) * unit
    smt_rows = (taps + 1) * wide // LANES + width // LANES
    smt_rows = -(-smt_rows // 16) * 16
    parts = call(
        functools.partial(kernel_back, heads, inner_total),
        (*shared, *kept[:-1], stats),
        [
            ((length, width), bf16),
            ((length, width), bf16),
            ((width, inner), bf16),
            ((width, inner), bf16),
            ((inner, width), bf16),
            ((width * wide // LANES, LANES), bf16),
            ((sm_rows, LANES), f32),
            ((smt_rows, LANES), f32),
        ],
        [
            pltpu.VMEM((length, inner), bf16),
            pltpu.VMEM((length, inner), bf16),
            pltpu.VMEM((length, inner), bf16),
            pltpu.VMEM((length, wide + LANES), bf16),
            pltpu.VMEM((length + HEAD, inner), f32),
            pltpu.VMEM((length + HEAD, wide), f32),
            pltpu.VMEM((length, LANES), f32),
        ],
    )
    turned = d_bits[1:2] + d_bits[:1] + d_bits[2:]
    bits = [t_bits, t_bits, turned, d_bits, d_bits, t_bits + d_bits, d_bits, t_bits + d_bits]
    streams = [Stream(part, b) for part, b in zip(parts, bits)]
    result, grad_x, gz, gx, gwo, gbc, sm, smt = call(
        functools.partial(kernel_sums, streams, t_bits + d_bits),
        (tok, cot, norm_gain[None, :], *parts),
        [
            ((length, width), bf16),
            ((length, width), bf16),
            ((width, inner), f32),
            ((width, inner), f32),
            ((inner, width), f32),
            ((width, wide), f32),
            ((sm_rows, LANES), f32),
            ((smt_rows, LANES), f32),
        ],
        [shape for s in streams for shape in s.scratch()],
        collective_id=1,
        has_side_effects=True,
    )
    sizes = [heads * width, taps * inner, inner, inner, LANES, LANES, LANES]
    flat, at, cut = sm.reshape(-1), 0, []
    for size in sizes:
        cut.append(flat[at : at + size])
        at += size
    gdt, g_cx, g_cxb, g_gain, g_dtb, g_alog, g_skip = cut
    flat, at, cut = smt.reshape(-1), 0, []
    for size in (taps * wide, wide, width):
        cut.append(flat[at : at + size])
        at += size
    g_cbc, g_cbcb, g_ng = cut
    return (
        result.reshape(seqs, length, width),
        grad_x.reshape(seqs, length, width),
        g_ng,
        gz,
        gx,
        gbc,
        gdt.reshape(heads, width).T,
        g_cx.reshape(taps, inner),
        g_cxb,
        g_cbc.reshape(taps, wide),
        g_cbcb,
        g_dtb[:heads],
        g_alog[:heads],
        g_skip[:heads],
        g_gain,
        gwo,
    )


def solution(mesh):
    placed = (
        P("dp", None, None),
        P("dp", None, None),
        P(),
        P(None, "tensor"),
        P(None, "tensor"),
        P(),
        P(None, "tensor"),
        P(None, "tensor"),
        P("tensor"),
        P(),
        P(),
        P("tensor"),
        P("tensor"),
        P("tensor"),
        P("tensor"),
        P("tensor", None),
    )
    return jax.shard_map(
        per_device,
        mesh=mesh,
        in_specs=placed,
        out_specs=(
            P("dp", None, None),
            P("dp", None, None),
            P(),
            P(None, "tensor"),
            P(None, "tensor"),
            P(),
            P(None, "tensor"),
            P(None, "tensor"),
            P("tensor"),
            P(),
            P(),
            P("tensor"),
            P("tensor"),
            P("tensor"),
            P("tensor"),
            P("tensor", None),
        ),
        check_vma=False,
    )
```

```python
import functools

import jax
import jax.numpy as jnp
from jax import lax
from jax.experimental import pallas as pl
from jax.experimental.pallas import tpu as pltpu
from jax.sharding import PartitionSpec as P

Q = 256
LANES = 128
HEAD = 8
epsilon = 1e-05
highest = lax.Precision.HIGHEST
f32 = jnp.float32
bf16 = jnp.bfloat16
NN = ((1,), (0,))
NT = ((1,), (1,))
TN = ((0,), (0,))


def mm(a, b, dims=NN):
    return lax.dot_general(
        a.astype(bf16), b.astype(bf16), (dims, ((), ())), preferred_element_type=f32
    )


def exact(a, b, dims=NN):
    return lax.dot_general(a, b, (dims, ((), ())), precision=highest, preferred_element_type=f32)


def iota(shape, dim):
    return lax.broadcasted_iota(jnp.int32, shape, dim)


def spread_matrix(width, head_dim):
    return (iota((LANES, width), 1) // head_dim == iota((LANES, width), 0)).astype(f32)


def spread_rows(width, head_dim):
    return (iota((width, LANES), 0) // head_dim == iota((width, LANES), 1)).astype(f32)


def shifted(pad_ref, start, kernel_ref, bias_ref):
    taps = kernel_ref.shape[0]
    total = bias_ref[...] + jnp.zeros((Q, pad_ref.shape[1]), f32)
    for j in range(taps):
        total = total + kernel_ref[j : j + 1, :] * pad_ref[pl.ds(HEAD + start - taps + 1 + j, Q), :]
    return total


def softplus(v):
    return jnp.maximum(v, 0.0) + jnp.log1p(jnp.exp(-jnp.abs(v)))


def decays(dt_rows, hp_ref):
    pre = dt_rows + hp_ref[0:1, :]
    step = softplus(pre)
    rate = jnp.exp(hp_ref[1:2, :])
    log_decay = -step * rate
    lower = (iota((Q, Q), 0) >= iota((Q, Q), 1)).astype(f32)
    return pre, step, rate, log_decay, exact(lower, log_decay)


def lane_row(ref):
    lane = iota((1, LANES), 1)
    total = jnp.zeros((1, LANES), f32)
    for h in range(ref.shape[0]):
        total = jnp.where(lane == h, ref[h], total)
    return total


def setup(dtw, dtb, alog, skip, wdt_s, hp):
    wdt_s[...] = jnp.zeros(wdt_s.shape, bf16)
    wdt_s[0 : dtw.shape[0], :] = dtw[...]
    hp[...] = jnp.zeros(hp.shape, f32)
    for k, ref in enumerate((dtb, alog, skip)):
        hp[k : k + 1, :] = lane_row(ref)


class Row:
    def __init__(self, ref):
        self.ref = ref

    def __getitem__(self, index):
        return self.ref[...][None, :]


def kernel_front(
    heads, tok, cot, ng, wz, wx, wbc, dtw, cx, cxb, cbc, cbcb, dtb, alog, dskip, gg, wo,
    normed_o, gate_o, x_o, bc_o, dt_o, cum_o, state_o, mixed_o, dgn_o, stats_o,
    wdt_s, hp,
):
    setup(dtw, dtb, alog, dskip, wdt_s, hp)
    ng, cxb, cbcb, gg = Row(ng), Row(cxb), Row(cbcb), Row(gg)
    length, inner = mixed_o.shape
    states = cbc.shape[1] // 2
    head_dim = inner // heads
    per = LANES // head_dim
    spread = spread_matrix(inner, head_dim)
    x_o[0:HEAD, :] = jnp.zeros((HEAD, inner), f32)
    bc_o[0:HEAD, :] = jnp.zeros((HEAD, 2 * states), f32)
    causal = iota((Q, Q), 0) >= iota((Q, Q), 1)
    lane = iota((Q, LANES), 1)
    chunks = length // Q
    for c in range(chunks):
        rows = pl.ds(c * Q, Q)
        t = tok[rows, :].astype(f32)
        n = t * lax.rsqrt(jnp.mean(t * t, axis=-1, keepdims=True) + epsilon) * ng[...]
        n = n.astype(bf16)
        normed_o[rows, :] = n
        gate_o[rows, :] = mm(n, wz[...])
        x_o[pl.ds(HEAD + c * Q, Q), :] = mm(n, wx[...])
        bc_o[pl.ds(HEAD + c * Q, Q), :] = mm(n, wbc[...])
        dt_o[rows, :] = mm(n, wdt_s[...], NT)
        dgn_o[rows, :] = mm(cot[rows, :], wo[...], NT)
    state_o[0] = jnp.zeros((inner, states), f32)
    for c in range(chunks):
        rows = pl.ds(c * Q, Q)
        v = shifted(x_o, c * Q, cx, cxb)
        xc = v * jax.nn.sigmoid(v)
        v = shifted(bc_o, c * Q, cbc, cbcb)
        bcc = v * jax.nn.sigmoid(v)
        b = bcc[:, :states].astype(bf16)
        cc = bcc[:, states:].astype(bf16)
        _, step, _, _, cum = decays(dt_o[rows, :], hp)
        cum_o[rows, :] = cum
        cum_t = jnp.transpose(cum)
        u = xc * exact(step, spread)
        scores = mm(cc, b, NT)
        outs = []
        for g in range(inner // LANES):
            part = u[:, g * LANES : (g + 1) * LANES]
            acc = jnp.zeros((Q, LANES), f32)
            for k in range(per):
                h = g * per + k
                e = jnp.exp(jnp.where(causal, cum[:, h : h + 1] - cum_t[h : h + 1, :], -1e30))
                acc = acc + mm(scores * e, jnp.where(lane // head_dim == k, part, 0.0))
            outs.append(acc)
        mixed = jnp.concatenate(outs, axis=1)
        if c > 0:
            mixed = mixed + mm(cc, state_o[c], NT) * exact(jnp.exp(cum), spread)
        if c + 1 < chunks:
            last = cum[Q - 1 : Q, :]
            tail = u * exact(jnp.exp(last - cum), spread)
            update = mm(tail, b, TN)
            if c > 0:
                rowdec = jnp.sum(
                    spread_rows(inner, head_dim) * jnp.exp(last), axis=1, keepdims=True
                )
                update = update + state_o[c] * rowdec
            state_o[c + 1] = update
        skip = jnp.sum(spread * hp_skip_col(hp), axis=0, keepdims=True)
        mixed = mixed + skip * xc
        mixed_o[rows, :] = mixed
        gate = gate_o[rows, :]
        gated = mixed * (gate * jax.nn.sigmoid(gate))
        sq = jnp.sum(gated * gated, axis=1, keepdims=True)
        pr = jnp.sum(gg[...] * dgn_o[rows, :] * gated, axis=1, keepdims=True)
        both = jnp.where(lane == 0, sq, jnp.where(lane == 1, pr, 0.0))
        stats_o[:, c * Q : (c + 1) * Q] = jnp.transpose(both)[0:8, :]


def hp_skip_col(hp):
    wide = jnp.where(iota((LANES, LANES), 0) == iota((LANES, LANES), 1), hp[2:3, :], 0.0)
    return jnp.sum(wide, axis=1, keepdims=True)


def put_rows(ref, start, value):
    count = value.shape[1] // LANES
    for r in range(value.shape[0]):
        for k in range(count):
            at = start + r * count + k
            ref[at : at + 1, :] = value[r : r + 1, k * LANES : (k + 1) * LANES]
    return start + value.shape[0] * count


def kernel_back(
    heads, inner_total, tok, cot, ng, wz, wx, wbc, dtw, cx, cxb, cbc, cbcb, dtb, alog, dskip, gg, wo,
    normed, gate_r, x_r, bc_r, dt_r, cum_r, state_r, mixed_r, dgn_r, stats,
    res_o, dn_o, gz_o, gx_o, gwo_o, gbc_o, sm_o, smt_o,
    gn_s, dz_s, dx_s, dbc_s, ddt_s, dvx_s, dvbc_s, inv_s, wdt_s, hp,
):
    setup(dtw, dtb, alog, dskip, wdt_s, hp)
    cxb, cbcb, gg = Row(cxb), Row(cbcb), Row(gg)
    length, inner = mixed_r.shape
    states = cbc.shape[1] // 2
    head_dim = inner // heads
    per = LANES // head_dim
    taps = cx.shape[0]
    spread = spread_matrix(inner, head_dim)
    spread_r = spread_rows(inner, head_dim)
    causal = iota((Q, Q), 0) >= iota((Q, Q), 1)
    lower = causal.astype(f32)
    lane = iota((Q, LANES), 1)
    skip = jnp.sum(spread * hp_skip_col(hp), axis=0, keepdims=True)
    dvx_s[pl.ds(length, HEAD), :] = jnp.zeros((HEAD, inner), f32)
    dvbc_s[pl.ds(length, HEAD), :] = jnp.zeros((HEAD, 2 * states), f32)
    chunks = length // Q
    for c in range(chunks):
        block = jnp.concatenate(
            [stats[:, c * Q : (c + 1) * Q], jnp.zeros((LANES - 8, Q), f32)], axis=0
        )
        inv_s[pl.ds(c * Q, Q), :] = jnp.transpose(block)
    g_gain = jnp.zeros((1, inner), f32)
    g_skip = jnp.zeros((1, inner), f32)
    g_alog = jnp.zeros((1, LANES), f32)
    g_dtb = jnp.zeros((1, LANES), f32)
    g_cx = [jnp.zeros((1, inner), f32) for _ in range(taps)]
    g_cxb = jnp.zeros((1, inner), f32)
    g_cbc = [jnp.zeros((1, 2 * states), f32) for _ in range(taps)]
    g_cbcb = jnp.zeros((1, 2 * states), f32)
    d_state = None
    for c in reversed(range(chunks)):
        rows = pl.ds(c * Q, Q)
        gate = gate_r[rows, :]
        mixed = mixed_r[rows, :]
        sg = jax.nn.sigmoid(gate)
        act = gate * sg
        gated = mixed * act
        inv = lax.rsqrt(inv_s[rows, :][:, 0:1] / inner_total + epsilon)
        pm = inv_s[rows, :][:, 1:2] / inner_total
        dgn = dgn_r[rows, :]
        normal = gated * inv
        gn_s[rows, :] = (normal * gg[...]).astype(bf16)
        g_gain = g_gain + jnp.sum(dgn * normal, axis=0, keepdims=True)
        dg = inv * (gg[...] * dgn) - gated * (inv * inv * inv) * pm
        dy = dg * act
        dz_s[rows, :] = (dg * mixed * (sg * (1.0 + gate * (1.0 - sg)))).astype(bf16)

        vx = shifted(x_r, c * Q, cx, cxb)
        sx = jax.nn.sigmoid(vx)
        xc = vx * sx
        vb = shifted(bc_r, c * Q, cbc, cbcb)
        sb = jax.nn.sigmoid(vb)
        bcc = vb * sb
        b = bcc[:, :states].astype(bf16)
        cc = bcc[:, states:].astype(bf16)
        pre = dt_r[rows, :] + hp[0:1, :]
        step = softplus(pre)
        rate = jnp.exp(hp[1:2, :])
        log_decay = -step * rate
        cum = cum_r[rows, :]
        cum_t = jnp.transpose(cum)
        stepw = exact(step, spread)
        u = xc * stepw
        scores = mm(cc, b, NT)
        d_scores = jnp.zeros((Q, Q), f32)
        d_cum = jnp.zeros((Q, LANES), f32)
        cols = jnp.zeros((8, Q), f32)
        dus = []
        for g in range(inner // LANES):
            up = u[:, g * LANES : (g + 1) * LANES].astype(bf16)
            dyp = dy[:, g * LANES : (g + 1) * LANES]
            acc = jnp.zeros((Q, LANES), f32)
            for k in range(per):
                h = g * per + k
                e = jnp.exp(jnp.where(causal, cum[:, h : h + 1] - cum_t[h : h + 1, :], -1e30))
                p = scores * e
                dyh = jnp.where(lane // head_dim == k, dyp, 0.0).astype(bf16)
                dp = mm(dyh, up, NT)
                d_scores = d_scores + dp * e
                gp = dp * p
                d_cum = d_cum + jnp.where(lane == h, jnp.sum(gp, axis=1, keepdims=True), 0.0)
                cols = cols + jnp.where(
                    iota((8, Q), 0) == h, jnp.sum(gp, axis=0, keepdims=True), 0.0
                )
                acc = acc + mm(p, dyh, TN)
            dus.append(acc)
        du = jnp.concatenate(dus, axis=1)
        d_cum = d_cum - jnp.transpose(
            jnp.concatenate([cols, jnp.zeros((LANES - 8, Q), f32)], axis=0)
        )
        d_c = mm(d_scores, b)
        d_b = mm(d_scores, cc, TN)
        d_prev = None
        if c > 0:
            state = state_r[c]
            decayed = exact(jnp.exp(cum), spread)
            dz = dy * decayed
            carried = mm(cc, state, NT) * dz
            d_cum = d_cum + exact(carried, spread, NT)
            d_c = d_c + mm(dz, state)
            d_prev = mm(dz, cc, TN)
        if d_state is not None:
            last = cum[Q - 1 : Q, :]
            tailw = exact(jnp.exp(last - cum), spread)
            ut = u * tailw
            dut = mm(b, d_state, NT)
            d_b = d_b + mm(ut, d_state)
            du = du + dut * tailw
            q = exact(dut * ut, spread, NT)
            d_last = jnp.sum(q, axis=0, keepdims=True)
            if c > 0:
                rowdec = jnp.sum(spread_r * jnp.exp(last), axis=1, keepdims=True)
                r = jnp.sum(d_state * state_r[c], axis=1, keepdims=True) * rowdec
                d_last = d_last + jnp.sum(spread_r * r, axis=0, keepdims=True)
                d_prev = d_prev + d_state * rowdec
            d_cum = d_cum - q + jnp.where(iota((Q, LANES), 0) == Q - 1, d_last, 0.0)
        d_state = d_prev
        d_log = exact(lower, d_cum, TN)
        g_alog = g_alog + jnp.sum(d_log * log_decay, axis=0, keepdims=True)
        d_step = exact(du * xc, spread, NT) - d_log * rate
        d_pre = d_step * jax.nn.sigmoid(pre)
        d_pre = jnp.where(lane < heads, d_pre, 0.0)
        g_dtb = g_dtb + jnp.sum(d_pre, axis=0, keepdims=True)
        g_skip = g_skip + jnp.sum(dy * xc, axis=0, keepdims=True)
        dxc = du * stepw + skip * dy
        dvx = dxc * (sx * (1.0 + vx * (1.0 - sx)))
        dvb = jnp.concatenate([d_b, d_c], axis=1) * (sb * (1.0 + vb * (1.0 - sb)))
        dvx_s[rows, :] = dvx
        dvbc_s[rows, :] = dvb
        g_cxb = g_cxb + jnp.sum(dvx, axis=0, keepdims=True)
        g_cbcb = g_cbcb + jnp.sum(dvb, axis=0, keepdims=True)
        dx = jnp.zeros((Q, inner), f32)
        dbc = jnp.zeros((Q, 2 * states), f32)
        for j in range(taps):
            back = pl.ds(c * Q + taps - 1 - j, Q)
            ahead = pl.ds(HEAD + c * Q - taps + 1 + j, Q)
            dx = dx + cx[j : j + 1, :] * dvx_s[back, :]
            dbc = dbc + cbc[j : j + 1, :] * dvbc_s[back, :]
            g_cx[j] = g_cx[j] + jnp.sum(dvx * x_r[ahead, :], axis=0, keepdims=True)
            g_cbc[j] = g_cbc[j] + jnp.sum(dvb * bc_r[ahead, :], axis=0, keepdims=True)
        dx_s[rows, :] = dx.astype(bf16)
        dbc_s[rows, :] = dbc.astype(bf16)
        ddt_s[rows, :] = d_pre.astype(bf16)

    g_ng = jnp.zeros((1, tok.shape[1]), f32)
    for c in range(chunks):
        rows = pl.ds(c * Q, Q)
        res_o[rows, :] = mm(gn_s[rows, :], wo[...]).astype(bf16)
        dn = mm(dz_s[rows, :], wz[...], NT) + mm(dx_s[rows, :], wx[...], NT)
        dn = dn + mm(dbc_s[rows, :], wbc[...], NT) + mm(ddt_s[rows, :], wdt_s[...])
        dn_o[rows, :] = dn.astype(bf16)
        t = tok[rows, :].astype(f32)
        unit = t * lax.rsqrt(jnp.mean(t * t, axis=-1, keepdims=True) + epsilon)
        g_ng = g_ng + jnp.sum(dn * unit, axis=0, keepdims=True)
    gz_o[...] = mm(normed[...], dz_s[...], TN).astype(bf16)
    gx_o[...] = mm(normed[...], dx_s[...], TN).astype(bf16)
    gw = mm(gn_s[...], cot[...], TN).astype(bf16)
    for k in range(gw.shape[1] // inner):
        gwo_o[pl.ds(k * inner, inner), :] = gw[:, k * inner : (k + 1) * inner]
    gb = mm(normed[...], dbc_s[...], TN).astype(bf16)
    width = gb.shape[0]
    for k in range(2 * states // LANES):
        gbc_o[pl.ds(k * width, width), :] = gb[:, k * LANES : (k + 1) * LANES]
    gdt = mm(ddt_s[...], normed[...], TN)
    sm_o[...] = jnp.zeros(sm_o.shape, f32)
    smt_o[...] = jnp.zeros(smt_o.shape, f32)
    at = put_rows(sm_o, 0, gdt[0:heads, :])
    for row in (*g_cx, g_cxb, g_gain):
        at = put_rows(sm_o, at, row)
    for row in (g_dtb, g_alog, exact(g_skip, spread, NT)):
        at = put_rows(sm_o, at, row)
    at = 0
    for row in (*g_cbc, g_cbcb, g_ng):
        at = put_rows(smt_o, at, row)


class Stream:
    def __init__(self, src, bits, start=0, rows=None, delay=0):
        self.start, self.delay = start, delay
        rows, self.lanes = rows or src.shape[0], src.shape[1]
        self.rows, self.dtype, self.bits = rows, src.dtype, bits
        tile = 32 // jnp.dtype(src.dtype).itemsize
        self.halve = []
        for _ in bits:
            split = rows % (2 * tile) == 0
            self.halve.append(split)
            if split:
                rows //= 2
        self.copies = len(bits) + sum(self.halve)

    def scratch(self):
        rows, shapes = self.rows, []
        shapes.append(pltpu.VMEM((self.rows, self.lanes), self.dtype))
        shapes.append(pltpu.VMEM((self.rows, self.lanes), self.dtype))
        shapes.append(pltpu.SemaphoreType.DMA((self.copies,)))
        shapes.append(pltpu.SemaphoreType.DMA((self.copies,)))
        for split in self.halve:
            if split:
                rows //= 2
            shapes.append(pltpu.VMEM((rows, self.lanes), self.dtype))
        return shapes


def run_stream(stream, src, refs):
    acc, out, send, recv = refs[:4]
    slots = refs[4:]
    src = src.at[pl.ds(stream.start, stream.rows), :]
    off, size, ref = 0, stream.rows, src
    trail = []
    sem = 0
    tile = 32 // jnp.dtype(stream.dtype).itemsize

    def place(v):
        return v if isinstance(v, int) else pl.multiple_of(v, tile)

    last = len(stream.bits) - 1
    for k, ((axis, bit), split) in enumerate(zip(stream.bits, stream.halve)):
        me = lax.axis_index(axis)
        side = lax.rem(me // bit, 2)
        peer = me + bit - 2 * bit * side
        if split:
            half = size // 2
            keep, give = off + side * half, off + (1 - side) * half
            trail.append((axis, peer, off))
        else:
            half, keep, give = size, off, off
        copy = pltpu.make_async_remote_copy(
            src_ref=ref.at[pl.ds(place(give), half), :],
            dst_ref=slots[k],
            send_sem=send.at[sem],
            recv_sem=recv.at[sem],
            device_id={axis: peer},
            device_id_type=pl.DeviceIdType.MESH,
        )
        sem += 1
        copy.start()
        yield
        copy.wait()
        rows = pl.ds(place(keep), half)
        target = out if k == last else acc
        total = ref[rows, :].astype(f32) + slots[k][...].astype(f32)
        target[rows, :] = total.astype(stream.dtype)
        off, size, ref = keep, half, target
    for axis, peer, parent in reversed(trail):
        rows = pl.ds(place(off), size)
        copy = pltpu.make_async_remote_copy(
            src_ref=out.at[rows, :],
            dst_ref=out.at[rows, :],
            send_sem=send.at[sem],
            recv_sem=recv.at[sem],
            device_id={axis: peer},
            device_id_type=pl.DeviceIdType.MESH,
        )
        sem += 1
        copy.start()
        yield
        copy.wait()
        off, size = parent, size * 2


def greet(peers):
    barrier = pltpu.get_barrier_semaphore()
    for axis, bit in peers:
        me = lax.axis_index(axis)
        peer = me + bit - 2 * bit * lax.rem(me // bit, 2)
        pl.semaphore_signal(
            barrier, inc=1, device_id={axis: peer}, device_id_type=pl.DeviceIdType.MESH
        )
    pl.semaphore_wait(barrier, len(peers))


def run_all(streams, sources, scratch):
    running = []
    at = 0
    outs = []
    for stream, src in zip(streams, sources):
        count = 4 + len(stream.bits)
        refs = scratch[at : at + count]
        at += count
        outs.append(refs[1])
        running.append(run_stream(stream, src, refs))
    for r in running:
        next(r)
    tick = 0
    pending = list(zip(running, (s.delay for s in streams)))
    while pending:
        pending = [(r, d) for r, d in pending if tick < d or next(r, 1) is None]
        tick += 1
    return outs


def kernel_stats(axis, src, out, slots, send, recv):
    size = lax.axis_size(axis)
    me = lax.axis_index(axis)
    barrier = pltpu.get_barrier_semaphore()
    for d in range(1, size):
        pl.semaphore_signal(
            barrier,
            inc=1,
            device_id={axis: lax.rem(me + d, size)},
            device_id_type=pl.DeviceIdType.MESH,
        )
    pl.semaphore_wait(barrier, size - 1)
    copies = []
    for d in range(1, size):
        copy = pltpu.make_async_remote_copy(
            src_ref=src,
            dst_ref=slots.at[d - 1],
            send_sem=send.at[d - 1],
            recv_sem=recv.at[d - 1],
            device_id={axis: lax.rem(me + d, size)},
            device_id_type=pl.DeviceIdType.MESH,
        )
        copy.start()
        copies.append(copy)
    total = src[...]
    for d, copy in enumerate(copies):
        copy.wait()
        total = total + slots[d]
    out[...] = total


def kernel_sums(streams, sources, peers, *refs):
    count = max(sources) + 1
    srcs, outs, scratch = refs[:count], refs[count : 2 * count], refs[2 * count :]
    greet(peers)
    gathered = run_all(streams, [srcs[k] for k in sources], scratch)
    for stream, k, value in zip(streams, sources, gathered):
        outs[k][pl.ds(stream.start, stream.rows), :] = value[...]


def get_row(ref, at, width):
    count = width // LANES
    return jnp.concatenate([ref[at + k : at + k + 1, :] for k in range(count)], axis=1)


def kernel_finish(
    tok, cot, ng, a_res, a_dn, a_gz, a_gx, a_gwo, a_gbc, a_sm, a_smt,
    res_o, gt_o, ng_o, gz_o, gx_o, gbc_o, gdt_o, cx_o, cxb_o, cbc_o, cbcb_o,
    dtb_o, alog_o, skip_o, gain_o, gwo_o,
):
    ng = Row(ng)
    for c in range(tok.shape[0] // Q):
        rows = pl.ds(c * Q, Q)
        t = tok[rows, :].astype(f32)
        res_o[rows, :] = (t + a_res[rows, :].astype(f32)).astype(bf16)
        r = lax.rsqrt(jnp.mean(t * t, axis=-1, keepdims=True) + epsilon)
        gd = a_dn[rows, :].astype(f32) * ng[...]
        mean = jnp.mean(t * gd, axis=-1, keepdims=True)
        d = r * gd - t * (r * r * r) * mean
        gt_o[rows, :] = (cot[rows, :].astype(f32) + d).astype(bf16)
    gz_o[...] = a_gz[...].astype(f32)
    gx_o[...] = a_gx[...].astype(f32)
    inner = gwo_o.shape[0]
    for k in range(gwo_o.shape[1] // inner):
        gwo_o[:, k * inner : (k + 1) * inner] = a_gwo[pl.ds(k * inner, inner), :].astype(f32)
    width = gbc_o.shape[0]
    for k in range(gbc_o.shape[1] // LANES):
        gbc_o[:, k * LANES : (k + 1) * LANES] = a_gbc[pl.ds(k * width, width), :].astype(f32)
    at = 0
    for out in (gdt_o, cx_o):
        for r in range(out.shape[0]):
            out[r : r + 1, :] = get_row(a_sm, at, out.shape[1])
            at += out.shape[1] // LANES
    for out in (cxb_o, gain_o):
        out[...] = get_row(a_sm, at, out.shape[0])[0]
        at += out.shape[0] // LANES
    for out in (dtb_o, alog_o, skip_o):
        out[...] = a_sm[at, 0 : out.shape[0]]
        at += 1
    at = 0
    for r in range(cbc_o.shape[0]):
        cbc_o[r : r + 1, :] = get_row(a_smt, at, cbc_o.shape[1])
        at += cbc_o.shape[1] // LANES
    for out in (cbcb_o, ng_o):
        out[...] = get_row(a_smt, at, out.shape[0])[0]
        at += out.shape[0] // LANES


def call(body, args, outs, scratch=(), limit=40, **params):
    vmem = pl.BlockSpec(memory_space=pltpu.VMEM)
    smem = pl.BlockSpec(memory_space=pltpu.SMEM)
    return pl.pallas_call(
        body,
        out_shape=[jax.ShapeDtypeStruct(s, d) for s, d in outs],
        in_specs=[smem if a.ndim == 1 and a.shape[0] < LANES else vmem for a in args],
        out_specs=[vmem] * len(outs),
        scratch_shapes=list(scratch),
        compiler_params=pltpu.CompilerParams(vmem_limit_bytes=limit * 1024 * 1024, **params),
    )(*args)


def per_device(
    tokens, cotangent, norm_gain, w_z, w_x, w_bc, w_dt, conv_x, conv_x_bias, conv_bc,
    conv_bc_bias, dt_bias, a_log, d_skip, gate_gain, w_out,
):
    seqs, length, width = tokens.shape
    assert seqs == 1 and length % Q == 0
    heads = dt_bias.shape[0]
    inner = w_z.shape[1]
    wide = w_bc.shape[1]
    states = wide // 2
    taps = conv_x.shape[0]
    dp, tensor = lax.axis_size("dp"), lax.axis_size("tensor")
    inner_total = inner * tensor
    chunks = length // Q
    tok = tokens.reshape(length, width)
    cot = cotangent.reshape(length, width)
    shared = (
        tok, cot, norm_gain, w_z, w_x, w_bc, w_dt.T, conv_x, conv_x_bias, conv_bc,
        conv_bc_bias, dt_bias, a_log, d_skip, gate_gain, w_out,
    )
    own = [pltpu.VMEM((LANES, width), bf16), pltpu.VMEM((8, LANES), f32)]
    kept = call(
        functools.partial(kernel_front, heads),
        shared,
        [
            ((length, width), bf16),
            ((length, inner), f32),
            ((length + HEAD, inner), f32),
            ((length + HEAD, wide), f32),
            ((length, LANES), f32),
            ((length, LANES), f32),
            ((chunks, inner, states), f32),
            ((length, inner), f32),
            ((length, inner), f32),
            ((8, length), f32),
        ],
        own,
    )
    t_bits = [("tensor", 1 << k) for k in range(tensor.bit_length() - 1)]
    d_bits = [("dp", 1 << k) for k in range(dp.bit_length() - 1)]
    stats = kept[-1]
    (stats,) = call(
        functools.partial(kernel_stats, "tensor"),
        (stats,),
        [(stats.shape, f32)],
        [
            pltpu.VMEM((tensor - 1, *stats.shape), f32),
            pltpu.SemaphoreType.DMA((tensor - 1,)),
            pltpu.SemaphoreType.DMA((tensor - 1,)),
        ],
        limit=4,
        collective_id=0,
        has_side_effects=True,
    )
    sm_rows = heads * width // LANES + (taps + 2) * inner // LANES + 3
    unit = 8 * dp
    sm_rows = -(-sm_rows // unit) * unit
    smt_rows = (taps + 1) * wide // LANES + width // LANES
    smt_rows = -(-smt_rows // 16) * 16
    parts = call(
        functools.partial(kernel_back, heads, inner_total),
        (*shared, *kept[:-1], stats),
        [
            ((length, width), bf16),
            ((length, width), bf16),
            ((width, inner), bf16),
            ((width, inner), bf16),
            ((width, inner), bf16),
            ((width * wide // LANES, LANES), bf16),
            ((sm_rows, LANES), f32),
            ((smt_rows, LANES), f32),
        ],
        [
            pltpu.VMEM((length, inner), bf16),
            pltpu.VMEM((length, inner), bf16),
            pltpu.VMEM((length, inner), bf16),
            pltpu.VMEM((length, wide), bf16),
            pltpu.VMEM((length, LANES), bf16),
            pltpu.VMEM((length + HEAD, inner), f32),
            pltpu.VMEM((length + HEAD, wide), f32),
            pltpu.VMEM((length, LANES), f32),
            *own,
        ],
    )
    turned = d_bits[1:2] + d_bits[:1] + d_bits[2:]
    res, dn, gz, gx, gwo, gbc, sm, smt = parts
    half = width // 2
    plan = [
        (7, Stream(smt, t_bits + d_bits)),
        (5, Stream(gbc, t_bits + d_bits)),
        (6, Stream(sm, d_bits)),
        (2, Stream(gz, d_bits, 0, half)),
        (0, Stream(res, t_bits)),
        (2, Stream(gz, d_bits, half, half, 1)),
        (3, Stream(gx, d_bits, 0, half, 2)),
        (1, Stream(dn, t_bits, delay=2)),
        (3, Stream(gx, d_bits, half, half, 3)),
        (4, Stream(gwo, d_bits, 0, half, 4)),
        (4, Stream(gwo, turned, half, half, 4)),
    ]
    streams = [s for _, s in plan]
    sums = call(
        functools.partial(kernel_sums, streams, [k for k, _ in plan], t_bits + d_bits),
        parts,
        [(p.shape, p.dtype) for p in parts],
        [shape for s in streams for shape in s.scratch()],
        collective_id=1,
        has_side_effects=True,
    )
    outs = call(
        kernel_finish,
        (tok, cot, norm_gain, *sums),
        [
            ((length, width), bf16),
            ((length, width), bf16),
            ((width,), f32),
            ((width, inner), f32),
            ((width, inner), f32),
            ((width, wide), f32),
            ((heads, width), f32),
            ((taps, inner), f32),
            ((inner,), f32),
            ((taps, wide), f32),
            ((wide,), f32),
            ((heads,), f32),
            ((heads,), f32),
            ((heads,), f32),
            ((inner,), f32),
            ((inner, width), f32),
        ],
    )
    outs = list(outs)
    for k in range(2):
        outs[k] = outs[k].reshape(seqs, length, width)
    outs[6] = outs[6].T
    return tuple(outs)


def solution(mesh):
    placed = (
        P("dp", None, None),
        P("dp", None, None),
        P(),
        P(None, "tensor"),
        P(None, "tensor"),
        P(),
        P(None, "tensor"),
        P(None, "tensor"),
        P("tensor"),
        P(),
        P(),
        P("tensor"),
        P("tensor"),
        P("tensor"),
        P("tensor"),
        P("tensor", None),
    )
    return jax.shard_map(
        per_device,
        mesh=mesh,
        in_specs=placed,
        out_specs=(
            P("dp", None, None),
            P("dp", None, None),
            P(),
            P(None, "tensor"),
            P(None, "tensor"),
            P(),
            P(None, "tensor"),
            P(None, "tensor"),
            P("tensor"),
            P(),
            P(),
            P("tensor"),
            P("tensor"),
            P("tensor"),
            P("tensor"),
            P("tensor", None),
        ),
        check_vma=False,
    )
```
